1024 devices in a mesh: section: 16 (over y, x_lo), seqtp: 64 (over x_hi, z, core).
Axes of the slice: x: 8 (x_hi: 4, x_lo: 2; x = x_hi * 2 + x_lo), y: 8, z: 8, core: 2. Of those that a mesh axis runs over, the one named last changes fastest.
Arguments:
- saved_in: bfloat16 [16, 4, 128, 4096], P('section', None, 'seqtp'), may hold values from -40 to 40
- grad_in: bfloat16 [16, 128, 4096], P('section', 'seqtp'), may hold values from -6 to 6
- slot_table: int32 [16], P('section'), may hold values from 0 to 3
- gain: bfloat16 [16, 4096], P('section'), may hold values from 0.099609375 to 1.8984375
- w_gate: bfloat16 [4096, 24576], P(None, 'seqtp'), may hold values from -0.09375 to 0.09375
- w_up: bfloat16 [4096, 24576], P(None, 'seqtp'), may hold values from -0.09375 to 0.09375
- w_down: bfloat16 [24576, 4096], P('seqtp'), may hold values from -0.0390625 to 0.0390625
Outputs:
- grad_prev: bfloat16 [16, 128, 4096], P('section', 'seqtp')
The draws below stay inside these ranges and needn't reach their ends.
All inputs are finite; a program needn't handle non-finite values.
Results may differ from the reference program's by a relative error of at most 0.0052.
Values may be sent and summed in bfloat16 or wider, within the bound.
A program may use at most 64 MiB of HBM per device.

```python
import math
import jax
import jax.numpy as jnp
from jax import lax

D = 4096
FF = 24576
TOKENS = 128
SLOTS = 4
SECTIONS = 16


def scaled_activation(key, shape):
    key_normal, key_rows, key_cols = jax.random.split(key, 3)
    low_end = math.log(0.3)
    high_end = math.log(3.0)
    row_scale = jnp.exp(jax.random.uniform(key_rows, shape[:-1] + (1,), jnp.float32, low_end, high_end))
    col_scale = jnp.exp(jax.random.uniform(key_cols, (shape[-1],), jnp.float32, low_end, high_end))
    base_values = jax.random.normal(key_normal, shape, jnp.float32)
    return jnp.clip(base_values * row_scale * col_scale, -40.0, 40.0)


def draw_saved_in(key, part):
    return scaled_activation(jax.random.fold_in(key, 23), (SECTIONS, SLOTS, TOKENS, D)).astype(jnp.bfloat16)


def draw_slot_table(key, part):
    key_values, key_place = jax.random.split(jax.random.fold_in(key, 37))
    values = jax.random.randint(key_values, (SECTIONS,), 0, SLOTS, jnp.int32)
    where_top = jax.random.randint(key_place, (), 0, SECTIONS, jnp.int32)
    values = values.at[where_top].set(SLOTS - 1)
    values = values.at[(where_top + 1) % SECTIONS].set(0)
    return values.astype(jnp.int32)


def steps_of(key, shape, cuts, low, high):
    loudness = 1.0
    for dim, parts in cuts:
        heights = jax.random.uniform(jax.random.fold_in(jax.random.fold_in(key, 6), dim), (parts,), jnp.float32, low / len(cuts), high / len(cuts))
        loudness = loudness * jnp.repeat(jnp.exp(heights), shape[dim] // parts).reshape((-1,) + (1,) * (len(shape) - 1 - dim))
    return loudness


def noise(key, extent, scale, reach, shards=(), dtype=jnp.bfloat16):
    values = scale * jax.random.normal(key, extent, jnp.float32)
    if shards:
        values = values * steps_of(key, extent, shards, -0.22, 0.18)
    return jnp.clip(values, -reach, reach).astype(dtype)


def setup_inputs(seed: int = 0) -> dict:
    splits = jax.random.split(jax.random.key(seed), 8)
    return {
        "saved_in": draw_saved_in(jax.random.fold_in(splits[7], 71), 0),
        "grad_in": noise(splits[1], (SECTIONS, TOKENS, D), 1.0, 6.0, ((0, 16), (1, 64))),
        "slot_table": draw_slot_table(jax.random.fold_in(splits[7], 71), 0),
        "gain": jnp.clip(1.0 + 0.18 * jax.random.normal(splits[3], (SECTIONS, D), jnp.float32), 0.099609375, 1.8984375).astype(jnp.bfloat16),
        "w_gate": noise(splits[4], (D, FF), D ** -0.5, 0.09375, ((1, 64),)),
        "w_up": noise(splits[5], (D, FF), D ** -0.5, 0.09375, ((1, 64),)),
        "w_down": noise(splits[6], (FF, D), FF ** -0.5, 0.0390625, ((0, 64),)),
    }


EPS = 1e-05

def rms_norm(values, gain_vec):
    wide = values.astype(jnp.float32)
    recip = lax.rsqrt(lax.optimization_barrier(jnp.mean(wide * wide, axis=-1, keepdims=True)) + EPS)
    return ((wide * recip * gain_vec).astype(jnp.bfloat16), recip)

def transposed(left, weight):
    return lax.dot_general(left, weight, (((1,), (1,)), ((), ())), preferred_element_type=jnp.float32)

def reference(saved_in, grad_in, slot_table, gain, w_gate, w_up, w_down):

    def one_section(operands):
        saved, cotangent, slot, gain_row = operands
        gain_vec = gain_row.astype(jnp.float32)
        behind = lax.dynamic_index_in_dim(saved, slot.astype(jnp.int32), 0, keepdims=False)
        normed_b, recip_b = rms_norm(behind, gain_vec)
        gate_b = jnp.dot(normed_b, w_gate, preferred_element_type=jnp.float32)
        up_b = jnp.dot(normed_b, w_up, preferred_element_type=jnp.float32)
        d_hidden = transposed(cotangent, w_down)
        probe = jax.nn.sigmoid(gate_b)
        d_gate = (d_hidden * up_b * probe * (1.0 + gate_b * (1.0 - probe))).astype(jnp.bfloat16)
        d_up = (d_hidden * gate_b * probe).astype(jnp.bfloat16)
        d_normed = transposed(d_gate, w_gate) + transposed(d_up, w_up)
        scaled = gain_vec * d_normed
        unit = behind.astype(jnp.float32) * recip_b
        grad_x = cotangent.astype(jnp.float32) + recip_b * (scaled - unit * lax.optimization_barrier(jnp.mean(scaled * unit, axis=-1, keepdims=True)))
        return grad_x.astype(jnp.bfloat16)
    grads = lax.map(one_section, (saved_in, grad_in, slot_table, gain))
    return jnp.roll(grads, -1, axis=0)
```

```python
import jax
import jax.numpy as jnp
from jax import lax
from jax.experimental import pallas as pl
from jax.experimental.pallas import tpu as pltpu
from jax.sharding import PartitionSpec as P

EPS = 1e-05
MESH = pl.DeviceIdType.MESH
NX, NZ, NC = 4, 8, 2
J = 4
BF, F32 = jnp.bfloat16, jnp.float32
OTHERS = [(dx, dc) for dx in (2, 1, 3, 0) for dc in (0, 1) if (dx, dc) != (0, 0)]


def nt(left, right):
    return lax.dot_general(left, right, (((1,), (1,)), ((), ())), preferred_element_type=F32)


def kernel(
    saved_ref, cot_ref, slot_ref, gain_ref, wg_hbm, wu_hbm, wd_hbm, out_ref,
    wgu, wd, own, first, x_buf, gu, dh, dboth, y_send, pair_buf, total, hop_buf, hop_send,
    t_send, t_recv, dn, grad_buf,
    w_sem, a_send, a_recv, ring_send, ring_recv, sib_send, sib_recv,
    pair_send, pair_recv, red_send, red_recv, t_ssem, t_rsem, out_ssem, out_rsem,
):
    sect = lax.axis_index("section")
    seq = lax.axis_index("seqtp")
    n_sect = lax.axis_size("section")
    xh, z, c = seq // (NZ * NC), lax.rem(seq // NC, NZ), lax.rem(seq, NC)
    width = x_buf.shape[-1]
    hidden = wd.shape[0]

    def at(dx, dz, dc):
        x2 = lax.rem(xh + dx + NX, NX)
        z2 = lax.rem(z + dz + NZ, NZ)
        c2 = lax.rem(c + dc, NC)
        return (sect, (x2 * NZ + z2) * NC + c2)

    after = (lax.rem(sect + 1, n_sect), seq)
    before = (lax.rem(sect + n_sect - 1, n_sect), seq)
    partners = [at(dx, 0, dc) for dx, dc in OTHERS] + [at(0, 1, 0), at(0, -1, 0), after, before]

    barrier = pltpu.get_barrier_semaphore()
    for who in partners:
        pl.semaphore_signal(barrier, inc=1, device_id=who, device_id_type=MESH)

    loads = [
        pltpu.make_async_copy(wg_hbm, wgu.at[:, pl.ds(0, hidden)], w_sem.at[0]),
        pltpu.make_async_copy(wu_hbm, wgu.at[:, pl.ds(hidden, hidden)], w_sem.at[1]),
        pltpu.make_async_copy(wd_hbm, wd, w_sem.at[2]),
    ]
    for load in loads:
        load.start()

    gain_vec = gain_ref[...].astype(F32)
    behind = saved_ref[0, slot_ref[0]].astype(F32)
    recip = lax.rsqrt(jnp.mean(behind * behind, axis=-1, keepdims=True) + EPS)
    normed = (behind * recip * gain_vec).astype(BF)
    for k in range(2 * J):
        own[k, 0] = normed[:, k * width : (k + 1) * width]
        own[k, 1] = cot_ref[0, :, k * width : (k + 1) * width]

    pl.semaphore_wait(barrier, len(partners))

    def half(dc):
        return lax.rem(c + dc, NC) * J

    for j in range(J):
        for dx, dc in OTHERS:
            pltpu.make_async_remote_copy(
                own.at[half(dc) + j],
                first.at[j, ((NX - dx) % NX) * NC + dc],
                a_send, a_recv.at[j], at(dx, 0, dc), MESH,
            ).start()
        first[j, 0] = own[half(0) + j]

    def rows(dz):
        return pl.ds(pl.multiple_of(lax.rem(z + dz + NZ, NZ) * 16, 16), 16)

    def hops(j, d):
        return 4 if (j + d) % 2 == 0 else 3

    def ring(j, d, h):
        sgn = 1 - 2 * d
        block = x_buf.at[half(0) + j, :, rows(-sgn * (h - 1))]
        return pltpu.make_async_remote_copy(
            block, block, ring_send, ring_recv.at[j, d, h - 1], at(0, sgn, 0), MESH
        )

    def ring_arrival(j, d, h):
        sgn = 1 - 2 * d
        block = x_buf.at[half(0) + j, :, rows(-sgn * h)]
        return pltpu.make_async_remote_copy(
            block, block, ring_send, ring_recv.at[j, d, h - 1], at(0, sgn, 0), MESH
        )

    def share(j, dz):
        block = x_buf.at[half(0) + j, :, rows(dz)]
        pltpu.make_async_remote_copy(
            block, block, sib_send, sib_recv.at[j], at(0, 0, 1), MESH
        ).start()

    for j in range(J):
        arrived = first.at[j, pl.ds(1, 7)]
        pltpu.make_async_remote_copy(
            arrived, arrived, a_send, a_recv.at[j], at(0, 0, 1), MESH
        ).wait_recv()
        for a in range(2):
            parts = [
                first[j, dx * NC + lax.rem(c2 + c, NC), a].astype(F32)
                for dx in range(NX) for c2 in range(NC)
            ]
            x_buf[half(0) + j, a, rows(0), :] = jnp.concatenate(parts, axis=0).astype(BF)
        ring(j, 0, 1).start()
        ring(j, 1, 1).start()
        share(j, 0)

    gu[...] = jnp.zeros_like(gu)
    dh[...] = jnp.zeros_like(dh)

    def first_products(k):
        cols = pl.ds(pl.multiple_of(k * width, width), width)
        gu[...] += jnp.dot(x_buf[k, 0], wgu[cols, :], preferred_element_type=F32)
        dh[...] += nt(x_buf[k, 1], wd[:, cols])

    for h in range(1, 5):
        for j in range(J):
            for d in range(2):
                if h <= hops(j, d):
                    ring_arrival(j, d, h).wait_recv()
                    if h < hops(j, d):
                        ring(j, d, h + 1).start()
                    share(j, -(1 - 2 * d) * h)
            if h == 4:
                if j == 0:
                    for load in loads:
                        load.wait()
                first_products(half(0) + j)
                theirs = x_buf.at[half(1) + j]
                pltpu.make_async_remote_copy(
                    theirs, theirs, sib_send, sib_recv.at[j], at(0, 0, 1), MESH
                ).wait_recv()
                first_products(half(1) + j)

    gate, up, hid = gu[:, :hidden], gu[:, hidden:], dh[...]
    probe = jax.nn.sigmoid(gate)
    dboth[:, :hidden] = (hid * up * probe * (1.0 + gate * (1.0 - probe))).astype(BF)
    dboth[:, hidden:] = (hid * gate * probe).astype(BF)

    def second_product(k):
        return nt(dboth[...], wgu[pl.ds(pl.multiple_of(k * width, width), width), :])

    def reduce_hop(j, d, h, src):
        return pltpu.make_async_remote_copy(
            src, hop_buf.at[j, d, h - 1], red_send, red_recv.at[j, d, h - 1],
            at(0, 1 - 2 * d, 0), MESH,
        )

    def give(j):
        y_send[j] = second_product(half(1) + j).astype(BF)
        pltpu.make_async_remote_copy(
            y_send.at[j], pair_buf.at[j], pair_send, pair_recv.at[j], at(0, 0, 1), MESH
        ).start()

    def join(j):
        pltpu.make_async_remote_copy(
            y_send.at[j], pair_buf.at[j], pair_send, pair_recv.at[j], at(0, 0, 1), MESH
        ).wait_recv()
        total[j] += pair_buf[j].astype(F32)
        for d in range(2):
            sgn = 1 - 2 * d
            hop_send[j, d] = total[j, rows(sgn * hops(j, d)), :].astype(BF)
            reduce_hop(j, d, 1, hop_send.at[j, d]).start()

    def turn(j, h):
        for d in range(2):
            sgn = 1 - 2 * d
            last = hops(j, d)
            if h > last:
                continue
            reduce_hop(j, d, h, hop_buf.at[j, d, h - 1]).wait_recv()
            if h < last:
                hop_buf[j, d, h - 1] = (
                    hop_buf[j, d, h - 1].astype(F32) + total[j, rows(sgn * (last - h)), :]
                ).astype(BF)
                reduce_hop(j, d, h + 1, hop_buf.at[j, d, h - 1]).start()
        if h == 4:
            mine = total[j, rows(0), :]
            for d in range(2):
                mine = mine + hop_buf[j, d, hops(j, d) - 1].astype(F32)
            for dx in range(NX):
                for c2 in range(NC):
                    r = dx * 4 + c2 * 2
                    t_send[j, dx, c2] = mine[r : r + 2].astype(BF)
            for dx, dc in OTHERS:
                pltpu.make_async_remote_copy(
                    t_send.at[j, dx, lax.rem(c + dc, NC)],
                    t_recv.at[j, ((NX - dx) % NX) * NC + dc],
                    t_ssem, t_rsem.at[j], at(dx, 0, dc), MESH,
                ).start()

    give(0)
    total[0] = second_product(half(0))
    give(1)
    join(0)
    total[1] = second_product(half(0) + 1)
    give(2)
    join(1)
    total[2] = second_product(half(0) + 2)
    give(3)
    turn(0, 1)
    join(2)
    total[3] = second_product(half(0) + 3)
    turn(1, 1)
    join(3)
    for j, h in ((0, 2), (2, 1), (1, 2), (3, 1), (0, 3), (2, 2), (1, 3), (3, 2), (0, 4), (2, 3), (1, 4), (3, 3), (2, 4), (3, 4)):
        turn(j, h)

    for j in range(J):
        arrived = t_recv.at[j, pl.ds(1, 7)]
        pltpu.make_async_remote_copy(
            arrived, arrived, t_ssem, t_rsem.at[j], at(0, 0, 1), MESH
        ).wait_recv()
        mine = t_send[j, 0, c].astype(F32)
        for dx in range(1, NX):
            mine = mine + t_recv[j, dx * NC].astype(F32)
        theirs = t_recv[j, 1].astype(F32)
        for dx in range(1, NX):
            theirs = theirs + t_recv[j, dx * NC + 1].astype(F32)
        dn[half(0) + j] = mine
        dn[half(1) + j] = theirs

    d_normed = jnp.concatenate([dn[k] for k in range(2 * J)], axis=1)
    scaled = gain_vec * d_normed
    unit = saved_ref[0, slot_ref[0]].astype(F32) * recip
    grad = cot_ref[0].astype(F32) + recip * (
        scaled - unit * jnp.mean(scaled * unit, axis=-1, keepdims=True)
    )
    grad_buf[0] = grad.astype(BF)
    result = pltpu.make_async_remote_copy(grad_buf, out_ref, out_ssem, out_rsem, before, MESH)
    result.start()

    def drain(ref, sem):
        pltpu.make_async_copy(ref, ref, sem).wait()

    drain(first.at[:, pl.ds(1, 7)], a_send)
    drain(x_buf.at[pl.ds(0, J), :, pl.ds(0, 7 * 16)], ring_send)
    drain(x_buf.at[pl.ds(0, J)], sib_send)
    drain(pair_buf, pair_send)
    drain(hop_buf.at[:, pl.ds(0, 1)], red_send)
    drain(hop_buf.at[:, pl.ds(0, 1), pl.ds(0, 3)], red_send)
    drain(t_recv.at[:, pl.ds(1, 7)], t_ssem)
    result.wait()


def on_device(saved_in, grad_in, slot_table, gain, w_gate, w_up, w_down):
    d, hidden = w_gate.shape
    width = d // (2 * J)
    tokens = NX * NZ * NC * 2
    vmem = pl.BlockSpec(memory_space=pltpu.VMEM)
    hbm = pl.BlockSpec(memory_space=pl.ANY)
    dma = pltpu.SemaphoreType.DMA
    return pl.pallas_call(
        kernel,
        out_shape=jax.ShapeDtypeStruct(grad_in.shape, BF),
        in_specs=[vmem, vmem, pl.BlockSpec(memory_space=pltpu.SMEM), vmem, hbm, hbm, hbm],
        out_specs=hbm,
        scratch_shapes=[
            pltpu.VMEM((d, 2 * hidden), BF),
            pltpu.VMEM((hidden, d), BF),
            pltpu.VMEM((2 * J, 2, 2, width), BF),
            pltpu.VMEM((J, NX * NC, 2, 2, width), BF),
            pltpu.VMEM((2 * J, 2, tokens, width), BF),
            pltpu.VMEM((tokens, 2 * hidden), F32),
            pltpu.VMEM((tokens, hidden), F32),
            pltpu.VMEM((tokens, 2 * hidden), BF),
            pltpu.VMEM((J, tokens, width), BF),
            pltpu.VMEM((J, tokens, width), BF),
            pltpu.VMEM((J, tokens, width), F32),
            pltpu.VMEM((J, 2, 4, 16, width), BF),
            pltpu.VMEM((J, 2, 16, width), BF),
            pltpu.VMEM((J, NX, NC, 2, width), BF),
            pltpu.VMEM((J, NX * NC, 2, width), BF),
            pltpu.VMEM((2 * J, 2, width), F32),
            pltpu.VMEM(grad_in.shape, BF),
            dma((3,)), dma, dma((J,)), dma, dma((J, 2, 4)), dma, dma((J,)),
            dma, dma((J,)), dma, dma((J, 2, 4)), dma, dma((J,)), dma, dma,
        ],
        compiler_params=pltpu.CompilerParams(
            collective_id=0, has_side_effects=True, vmem_limit_bytes=40 * 1024 * 1024
        ),
    )(saved_in, grad_in, slot_table, gain, w_gate, w_up, w_down)


def solution(mesh):
    return jax.shard_map(
        on_device,
        mesh=mesh,
        in_specs=(
            P("section", None, "seqtp", None),
            P("section", "seqtp", None),
            P("section"),
            P("section", None),
            P(None, "seqtp"),
            P(None, "seqtp"),
            P("seqtp", None),
        ),
        out_specs=P("section", "seqtp", None),
        check_vma=False,
    )
```

```python
import jax
import jax.numpy as jnp
from jax import lax
from jax.experimental import pallas as pl
from jax.experimental.pallas import tpu as pltpu
from jax.sharding import PartitionSpec as P

EPS = 1e-05
MESH = pl.DeviceIdType.MESH
NX, NZ, NC = 4, 8, 2
J = 4
G = 2
PER = J // G
BF, F32 = jnp.bfloat16, jnp.float32
ALL = [(dx, dc) for dx in (2, 1, 3, 0) for dc in (0, 1)]
BARRIER_Z = (1, -1)
ORDER = (
    (1, 2, 7, 6, 3, 5, 4),
    (1, 7, 2, 6, 3, 5, 4),
    (7, 1, 2, 6, 3, 5, 4),
    (7, 6, 1, 2, 5, 3, 4),
    (7, 6, 1, 5, 2, 3, 4),
    (7, 6, 1, 5, 2, 3, 4),
    (7, 1, 6, 2, 5, 3, 4),
    (1, 7, 2, 6, 3, 5, 4),
)
OTHERS = [(dx, dc) for dx in (2, 1, 3, 0) for dc in (0, 1) if (dx, dc) != (0, 0)]


def nt(left, right):
    return lax.dot_general(left, right, (((1,), (1,)), ((), ())), preferred_element_type=F32)


def kernel(
    saved_hbm, cot_hbm, slot_ref, gain_hbm, wg_hbm, wu_hbm, wd_hbm, out_ref,
    saved, cot, gain, picked, saved_next, cot_next, gain_next,
    wgu, wd, own, first, x_buf, gu, dh, dboth, y_send, pair_buf, total, r_send, r_recv, m_send,
    t_send, t_recv, dn,
    in_sem, w_sem, next_send, next_recv, a_send, a_recv, z_send, z_recv, sib_send, sib_recv,
    pair_send, pair_recv, red_send, red_recv, t_ssem, t_rsem,
):
    sect = lax.axis_index("section")
    seq = lax.axis_index("seqtp")
    n_sect = lax.axis_size("section")
    xh, z, c = seq // (NZ * NC), lax.rem(seq // NC, NZ), lax.rem(seq, NC)
    width = x_buf.shape[-1]
    hidden = wd.shape[0]

    def at(dx, dz, dc, ds=0):
        x2 = lax.rem(xh + dx + NX, NX)
        z2 = lax.rem(z + dz + NZ, NZ)
        c2 = lax.rem(c + dc, NC)
        return (lax.rem(sect + ds + n_sect, n_sect), (x2 * NZ + z2) * NC + c2)

    partners = [at(dx, 0, dc) for dx, dc in OTHERS]
    partners += [at(0, dz, 0) for dz in BARRIER_Z]
    partners += [at(dx, 0, dc, ds) for ds in (1, -1) for dx, dc in ALL]

    inputs = [
        pltpu.make_async_copy(saved_hbm, saved, in_sem.at[0]),
        pltpu.make_async_copy(cot_hbm, cot, in_sem.at[1]),
        pltpu.make_async_copy(gain_hbm, gain, in_sem.at[2]),
    ]
    loads = [
        pltpu.make_async_copy(wg_hbm, wgu.at[:, pl.ds(0, hidden)], w_sem.at[0]),
        pltpu.make_async_copy(wu_hbm, wgu.at[:, pl.ds(hidden, hidden)], w_sem.at[1]),
        pltpu.make_async_copy(wd_hbm, wd, w_sem.at[2]),
    ]
    for load in inputs:
        load.start()
    barrier = pltpu.get_barrier_semaphore()
    for who in partners:
        pl.semaphore_signal(barrier, inc=1, device_id=who, device_id_type=MESH)
    for load in loads:
        load.start()
    for load in inputs:
        load.wait()

    def recip_of(values):
        return lax.rsqrt(jnp.mean(values * values, axis=-1, keepdims=True) + EPS)

    picked[...] = saved[0, slot_ref[0]]
    behind = picked[...].astype(F32)
    normed = (behind * recip_of(behind) * gain[...].astype(F32)).astype(BF)
    for k in range(2 * J):
        own[k, 0] = normed[:, k * width : (k + 1) * width]
        own[k, 1] = cot[0, :, k * width : (k + 1) * width]

    pl.semaphore_wait(barrier, len(partners))

    def half(dc):
        return lax.rem(c + dc, NC) * J

    for g in range(G):
        for dx, dc in OTHERS:
            pltpu.make_async_remote_copy(
                own.at[pl.ds(half(dc) + g * PER, PER)],
                first.at[g, ((NX - dx) % NX) * NC + dc],
                a_send, a_recv.at[g], at(dx, 0, dc), MESH,
            ).start()
        for i in range(PER):
            first[g, 0, i] = own[half(0) + g * PER + i]

    def ahead(i, src, dst):
        return pltpu.make_async_remote_copy(
            src, dst, next_send.at[i], next_recv.at[i], at(0, 0, 0, -1), MESH
        )

    handed = [ahead(0, picked, saved_next), ahead(1, cot, cot_next), ahead(2, gain, gain_next)]
    for copy in handed:
        copy.start()

    def rows(dz):
        return pl.ds(pl.multiple_of(lax.rem(z + dz + NZ, NZ) * 16, 16), 16)

    def push(j, origin, dz):
        block = x_buf.at[half(0) + j, :, rows(origin)]
        return pltpu.make_async_remote_copy(
            block, block, z_send, z_recv.at[j, lax.rem(origin - dz + NZ, NZ)], at(0, dz, 0), MESH
        )

    def arrival(j, origin):
        block = x_buf.at[half(0) + j, :, rows(origin)]
        pltpu.make_async_remote_copy(
            block, block, z_send, z_recv.at[j, origin], at(0, 1, 0), MESH
        ).wait_recv()

    def share(j, dz):
        block = x_buf.at[half(0) + j, :, rows(dz)]
        pltpu.make_async_remote_copy(
            block, block, sib_send, sib_recv.at[j], at(0, 0, 1), MESH
        ).start()

    for j in range(J):
        if j % PER == 0:
            arrived = first.at[j // PER, pl.ds(1, 7)]
            pltpu.make_async_remote_copy(
                arrived, arrived, a_send, a_recv.at[j // PER], at(0, 0, 1), MESH
            ).wait_recv()
        for a in range(2):
            parts = [
                first[j // PER, dx * NC + lax.rem(c2 + c, NC), j % PER, a].astype(F32)
                for dx in range(NX) for c2 in range(NC)
            ]
            x_buf[half(0) + j, a, rows(0), :] = jnp.concatenate(parts, axis=0).astype(BF)
        for dz in (1, -1):
            push(j, 0, dz).start()
        share(j, 0)

    gu[...] = jnp.zeros_like(gu)
    dh[...] = jnp.zeros_like(dh)

    def first_products(k):
        cols = pl.ds(pl.multiple_of(k * width, width), width)
        gu[...] += jnp.dot(x_buf[k, 0], wgu[cols, :], preferred_element_type=F32)
        dh[...] += nt(x_buf[k, 1], wd[:, cols])

    def handle(j, r):
        arrival(j, r)
        plus = r > NZ // 2
        end = (r == NZ // 2) | (r == (NZ // 2 + 1 if j % 2 else NZ // 2 - 1))

        @pl.when(jnp.logical_not(end))
        def _():
            push(j, r, jnp.where(plus, 1, -1)).start()

        share(j, r)

    for t in range(NZ - 1):
        r = sum(jnp.where(z == i, ORDER[i][t], 0) for i in range(NZ))
        for j in range(J):
            handle(j, r)
            if t == NZ - 2:
                if j == 0:
                    for load in loads:
                        load.wait()
                first_products(half(0) + j)
                theirs = x_buf.at[half(1) + j]
                pltpu.make_async_remote_copy(
                    theirs, theirs, sib_send, sib_recv.at[j], at(0, 0, 1), MESH
                ).wait_recv()
                first_products(half(1) + j)

    gate, up, hid = gu[:, :hidden], gu[:, hidden:], dh[...]
    probe = jax.nn.sigmoid(gate)
    dboth[:, :hidden] = (hid * up * probe * (1.0 + gate * (1.0 - probe))).astype(BF)
    dboth[:, hidden:] = (hid * gate * probe).astype(BF)

    def second_product(k):
        return nt(dboth[...], wgu[pl.ds(pl.multiple_of(k * width, width), width), :])

    def pair_copy(j):
        return pltpu.make_async_remote_copy(
            y_send.at[j], pair_buf.at[j], pair_send, pair_recv.at[j], at(0, 0, 1), MESH
        )

    def give(j):
        y_send[j] = second_product(half(1) + j).astype(BF)
        pair_copy(j).start()

    def reduce_copy(j, slot, src, dz):
        return pltpu.make_async_remote_copy(
            src, r_recv.at[j, slot], red_send, red_recv.at[j, slot], at(0, dz, 0), MESH
        )

    def landed(j, slot):
        reduce_copy(j, slot, r_recv.at[j, slot], 1).wait_recv()
        return r_recv[j, slot].astype(F32)

    def far(j):
        return 1 if j % 2 == 0 else -1

    def join(j):
        summed = second_product(half(0) + j)
        pair_copy(j).wait_recv()
        summed = summed + pair_buf[j].astype(F32)
        total[j] = summed
        r_send[j] = summed.astype(BF)
        reduce_copy(j, 2, r_send.at[j, rows(4)], 2 * far(j)).start()
        reduce_copy(j, 0, r_send.at[j, rows(3)], 1).start()
        reduce_copy(j, 1, r_send.at[j, rows(-3)], -1).start()
        reduce_copy(j, 3, r_send.at[j, rows(1)], 1).start()
        reduce_copy(j, 4, r_send.at[j, rows(-1)], -1).start()

    def merge(j):
        more = landed(j, 2)
        for i, sgn in ((0, 1), (1, -1)):
            block = total[j, rows(2 * sgn), :] + landed(j, i)
            if sgn == far(j):
                block = block + more
            m_send[j, i] = block.astype(BF)
            reduce_copy(j, 5 + i, m_send.at[j, i], 2 * sgn).start()

    def finish(j):
        block = total[j, rows(0), :]
        for slot in (3, 4, 5, 6):
            block = block + landed(j, slot)
        for dx in range(NX):
            for c2 in range(NC):
                r = dx * 4 + c2 * 2
                t_send[dx, c2, j] = block[r : r + 2].astype(BF)
        g = j // PER
        if j % PER == PER - 1:
            for dx, dc in ALL:
                pltpu.make_async_remote_copy(
                    t_send.at[dx, lax.rem(c + dc, NC), pl.ds(g * PER, PER)],
                    t_recv.at[g, ((NX - dx) % NX) * NC + dc],
                    t_ssem, t_rsem.at[g], at(dx, 0, dc, -1), MESH,
                ).start()

    give(0)
    give(1)
    join(0)
    give(2)
    join(1)
    give(3)
    join(2)
    join(3)
    for j in range(J):
        merge(j)
    for j in range(J):
        finish(j)

    for copy in handed:
        copy.wait_recv()
    behind = saved_next[...].astype(F32)
    recip = recip_of(behind)
    unit = behind * recip
    for j in range(J):
        g, i = j // PER, j % PER
        if i == 0:
            pltpu.make_async_remote_copy(
                t_recv.at[g], t_recv.at[g], t_ssem, t_rsem.at[g], at(0, 0, 1), MESH
            ).wait_recv()
        for dc in range(NC):
            part = t_recv[g, dc, i].astype(F32)
            for dx in range(1, NX):
                part = part + t_recv[g, dx * NC + dc, i].astype(F32)
            dn[half(dc) + j] = part

    d_normed = jnp.concatenate([dn[k] for k in range(2 * J)], axis=1)
    scaled = gain_next[...].astype(F32) * d_normed
    grad = cot_next[0].astype(F32) + recip * (
        scaled - unit * jnp.mean(scaled * unit, axis=-1, keepdims=True)
    )
    out_ref[0] = grad.astype(BF)

    def drain(ref, sem):
        pltpu.make_async_copy(ref, ref, sem).wait()

    for copy in handed:
        copy.wait_send()
    drain(first.at[:, pl.ds(1, 7)], a_send)
    drain(x_buf.at[pl.ds(0, J), :, pl.ds(0, 7 * 16)], z_send)
    drain(x_buf.at[pl.ds(0, J)], sib_send)
    drain(pair_buf, pair_send)
    drain(r_recv, red_send)
    drain(t_recv, t_ssem)


def on_device(saved_in, grad_in, slot_table, gain, w_gate, w_up, w_down):
    d, hidden = w_gate.shape
    width = d // (2 * J)
    tokens = NX * NZ * NC * 2
    hbm = pl.BlockSpec(memory_space=pltpu.HBM)
    dma = pltpu.SemaphoreType.DMA
    row = (saved_in.shape[2], d)
    return pl.pallas_call(
        kernel,
        out_shape=jax.ShapeDtypeStruct(grad_in.shape, BF),
        in_specs=[hbm, hbm, pl.BlockSpec(memory_space=pltpu.SMEM), hbm, hbm, hbm, hbm],
        out_specs=pl.BlockSpec(memory_space=pltpu.VMEM),
        scratch_shapes=[
            pltpu.VMEM(saved_in.shape, BF),
            pltpu.VMEM(grad_in.shape, BF),
            pltpu.VMEM(gain.shape, BF),
            pltpu.VMEM(row, BF),
            pltpu.VMEM(row, BF),
            pltpu.VMEM(grad_in.shape, BF),
            pltpu.VMEM(gain.shape, BF),
            pltpu.VMEM((d, 2 * hidden), BF),
            pltpu.VMEM((hidden, d), BF),
            pltpu.VMEM((2 * J, 2, 2, width), BF),
            pltpu.VMEM((G, NX * NC, PER, 2, 2, width), BF),
            pltpu.VMEM((2 * J, 2, tokens, width), BF),
            pltpu.VMEM((tokens, 2 * hidden), F32),
            pltpu.VMEM((tokens, hidden), F32),
            pltpu.VMEM((tokens, 2 * hidden), BF),
            pltpu.VMEM((J, tokens, width), BF),
            pltpu.VMEM((J, tokens, width), BF),
            pltpu.VMEM((J, tokens, width), F32),
            pltpu.VMEM((J, tokens, width), BF),
            pltpu.VMEM((J, NZ - 1, 16, width), BF),
            pltpu.VMEM((J, 2, 16, width), BF),
            pltpu.VMEM((NX, NC, J, 2, width), BF),
            pltpu.VMEM((G, NX * NC, PER, 2, width), BF),
            pltpu.VMEM((2 * J, 2, width), F32),
            dma((3,)), dma((3,)), dma((3,)), dma((3,)),
            dma, dma((G,)), dma, dma((J, NZ)), dma, dma((J,)),
            dma, dma((J,)), dma, dma((J, NZ - 1)), dma, dma((G,)),
        ],
        compiler_params=pltpu.CompilerParams(
            collective_id=0, has_side_effects=True, vmem_limit_bytes=60 * 1024 * 1024
        ),
    )(saved_in, grad_in, slot_table, gain, w_gate, w_up, w_down)


def solution(mesh):
    return jax.shard_map(
        on_device,
        mesh=mesh,
        in_specs=(
            P("section", None, "seqtp", None),
            P("section", "seqtp", None),
            P("section"),
            P("section", None),
            P(None, "seqtp"),
            P(None, "seqtp"),
            P("seqtp", None),
        ),
        out_specs=P("section", "seqtp", None),
        check_vma=False,
    )
```

```python
import jax
import jax.numpy as jnp
from jax import lax
from jax.experimental import pallas as pl
from jax.experimental.pallas import tpu as pltpu
from jax.sharding import PartitionSpec as P

EPS = 1e-05
MESH = pl.DeviceIdType.MESH
NX, NZ, NC = 4, 8, 2
J = 4
G = 4
PER = J // G
BF, F32 = jnp.bfloat16, jnp.float32
ALL = [(dx, dc) for dx in (2, 1, 3, 0) for dc in (0, 1)]
BARRIER_Z = (1, -1)
ORDER = (
    (1, 2, 7, 6, 3, 5, 4),
    (1, 7, 2, 6, 3, 5, 4),
    (7, 1, 2, 6, 3, 5, 4),
    (7, 6, 1, 2, 5, 3, 4),
    (7, 6, 1, 5, 2, 3, 4),
    (7, 6, 1, 5, 2, 3, 4),
    (7, 1, 6, 2, 5, 3, 4),
    (1, 7, 2, 6, 3, 5, 4),
)
OTHERS = [(dx, dc) for dx in (2, 1, 3, 0) for dc in (0, 1) if (dx, dc) != (0, 0)]


def nt(left, right):
    return lax.dot_general(left, right, (((1,), (1,)), ((), ())), preferred_element_type=F32)


def kernel(
    saved_hbm, cot_hbm, slot_ref, gain_hbm, wg_hbm, wu_hbm, wd_hbm, out_ref,
    saved, cot, gain, picked, saved_next, cot_next, gain_next,
    wgu, wd, own, first, x_buf, gu, dh, dboth, y_send, pair_buf, total, r_send, r_recv, m_send,
    t_send, t_recv, dn,
    in_sem, w_sem, next_send, next_recv, a_send, a_recv, z_send, z_recv, sib_send, sib_recv,
    pair_send, pair_recv, red_send, red_recv, t_ssem, t_rsem,
):
    sect = lax.axis_index("section")
    seq = lax.axis_index("seqtp")
    n_sect = lax.axis_size("section")
    xh, z, c = seq // (NZ * NC), lax.rem(seq // NC, NZ), lax.rem(seq, NC)
    width = x_buf.shape[-1]
    hidden = wd.shape[0]

    def at(dx, dz, dc, ds=0):
        x2 = lax.rem(xh + dx + NX, NX)
        z2 = lax.rem(z + dz + NZ, NZ)
        c2 = lax.rem(c + dc, NC)
        return (lax.rem(sect + ds + n_sect, n_sect), (x2 * NZ + z2) * NC + c2)

    partners = [at(dx, 0, dc) for dx, dc in OTHERS]
    partners += [at(0, dz, 0) for dz in BARRIER_Z]
    partners += [at(dx, 0, dc, ds) for ds in (1, -1) for dx, dc in ALL]

    inputs = [
        pltpu.make_async_copy(saved_hbm, saved, in_sem.at[0]),
        pltpu.make_async_copy(cot_hbm, cot, in_sem.at[1]),
        pltpu.make_async_copy(gain_hbm, gain, in_sem.at[2]),
    ]
    loads = [
        pltpu.make_async_copy(wg_hbm, wgu.at[:, pl.ds(0, hidden)], w_sem.at[0]),
        pltpu.make_async_copy(wu_hbm, wgu.at[:, pl.ds(hidden, hidden)], w_sem.at[1]),
        pltpu.make_async_copy(wd_hbm, wd, w_sem.at[2]),
    ]
    for load in inputs:
        load.start()
    barrier = pltpu.get_barrier_semaphore()
    for who in partners:
        pl.semaphore_signal(barrier, inc=1, device_id=who, device_id_type=MESH)
    for load in loads:
        load.start()
    for load in inputs:
        load.wait()

    def recip_of(values):
        return lax.rsqrt(jnp.mean(values * values, axis=-1, keepdims=True) + EPS)

    picked[...] = saved[0, slot_ref[0]]
    behind = picked[...].astype(F32)
    normed = (behind * recip_of(behind) * gain[...].astype(F32)).astype(BF)
    for k in range(2 * J):
        own[k, 0] = normed[:, k * width : (k + 1) * width]
        own[k, 1] = cot[0, :, k * width : (k + 1) * width]

    pl.semaphore_wait(barrier, len(partners))

    def half(dc):
        return lax.rem(c + dc, NC) * J

    for g in range(G):
        for dx, dc in OTHERS:
            pltpu.make_async_remote_copy(
                own.at[pl.ds(half(dc) + g * PER, PER)],
                first.at[g, ((NX - dx) % NX) * NC + dc],
                a_send, a_recv.at[g], at(dx, 0, dc), MESH,
            ).start()
        for i in range(PER):
            first[g, 0, i] = own[half(0) + g * PER + i]

    def ahead(i, src, dst):
        return pltpu.make_async_remote_copy(
            src, dst, next_send.at[i], next_recv.at[i], at(0, 0, 0, -1), MESH
        )

    handed = [ahead(0, picked, saved_next), ahead(1, cot, cot_next), ahead(2, gain, gain_next)]
    for copy in handed:
        copy.start()

    def rows(dz):
        return pl.ds(pl.multiple_of(lax.rem(z + dz + NZ, NZ) * 16, 16), 16)

    def push(j, origin, dz):
        block = x_buf.at[half(0) + j, :, rows(origin)]
        return pltpu.make_async_remote_copy(
            block, block, z_send, z_recv.at[j, lax.rem(origin - dz + NZ, NZ)], at(0, dz, 0), MESH
        )

    def arrival(j, origin):
        block = x_buf.at[half(0) + j, :, rows(origin)]
        pltpu.make_async_remote_copy(
            block, block, z_send, z_recv.at[j, origin], at(0, 1, 0), MESH
        ).wait_recv()

    def share(j, dz):
        block = x_buf.at[half(0) + j, :, rows(dz)]
        pltpu.make_async_remote_copy(
            block, block, sib_send, sib_recv.at[j], at(0, 0, 1), MESH
        ).start()

    for j in range(J):
        if j % PER == 0:
            arrived = first.at[j // PER, pl.ds(1, 7)]
            pltpu.make_async_remote_copy(
                arrived, arrived, a_send, a_recv.at[j // PER], at(0, 0, 1), MESH
            ).wait_recv()
        for a in range(2):
            parts = [
                first[j // PER, dx * NC + lax.rem(c2 + c, NC), j % PER, a].astype(F32)
                for dx in range(NX) for c2 in range(NC)
            ]
            x_buf[half(0) + j, a, rows(0), :] = jnp.concatenate(parts, axis=0).astype(BF)
        for dz in (1, -1):
            push(j, 0, dz).start()
    for j in range(J):
        share(j, 0)

    gu[...] = jnp.zeros_like(gu)
    dh[...] = jnp.zeros_like(dh)

    def first_products(k):
        cols = pl.ds(pl.multiple_of(k * width, width), width)
        gu[...] += jnp.dot(x_buf[k, 0], wgu[cols, :], preferred_element_type=F32)
        dh[...] += nt(x_buf[k, 1], wd[:, cols])

    def handle(j, r):
        arrival(j, r)
        plus = r > NZ // 2
        end = (r == NZ // 2) | (r == (NZ // 2 + 1 if j % 2 else NZ // 2 - 1))

        @pl.when(jnp.logical_not(end))
        def _():
            push(j, r, jnp.where(plus, 1, -1)).start()

        share(j, r)

    for t in range(NZ - 1):
        r = sum(jnp.where(z == i, ORDER[i][t], 0) for i in range(NZ))
        for j in range(J):
            handle(j, r)
            if t == NZ - 2:
                if j == 0:
                    for load in loads:
                        load.wait()
                first_products(half(0) + j)
                theirs = x_buf.at[half(1) + j]
                pltpu.make_async_remote_copy(
                    theirs, theirs, sib_send, sib_recv.at[j], at(0, 0, 1), MESH
                ).wait_recv()
                first_products(half(1) + j)

    gate, up, hid = gu[:, :hidden], gu[:, hidden:], dh[...]
    probe = jax.nn.sigmoid(gate)
    dboth[:, :hidden] = (hid * up * probe * (1.0 + gate * (1.0 - probe))).astype(BF)
    dboth[:, hidden:] = (hid * gate * probe).astype(BF)

    def second_product(k):
        return nt(dboth[...], wgu[pl.ds(pl.multiple_of(k * width, width), width), :])

    def pair_copy(j):
        return pltpu.make_async_remote_copy(
            y_send.at[j], pair_buf.at[j], pair_send, pair_recv.at[j], at(0, 0, 1), MESH
        )

    def give(j):
        y_send[j] = second_product(half(1) + j).astype(BF)
        pair_copy(j).start()

    def reduce_copy(j, slot, src, dz):
        return pltpu.make_async_remote_copy(
            src, r_recv.at[j, slot], red_send, red_recv.at[j, slot], at(0, dz, 0), MESH
        )

    def landed(j, slot):
        reduce_copy(j, slot, r_recv.at[j, slot], 1).wait_recv()
        return r_recv[j, slot].astype(F32)

    def far(j):
        return 1 if j % 2 == 0 else -1

    def join(j):
        summed = second_product(half(0) + j)
        pair_copy(j).wait_recv()
        summed = summed + pair_buf[j].astype(F32)
        total[j] = summed
        r_send[j] = summed.astype(BF)
        reduce_copy(j, 2, r_send.at[j, rows(4)], 2 * far(j)).start()
        reduce_copy(j, 0, r_send.at[j, rows(3)], 1).start()
        reduce_copy(j, 1, r_send.at[j, rows(-3)], -1).start()
        reduce_copy(j, 3, r_send.at[j, rows(1)], 1).start()
        reduce_copy(j, 4, r_send.at[j, rows(-1)], -1).start()

    def merge(j):
        more = landed(j, 2)
        for i, sgn in ((0, 1), (1, -1)):
            block = total[j, rows(2 * sgn), :] + landed(j, i)
            if sgn == far(j):
                block = block + more
            m_send[j, i] = block.astype(BF)
            reduce_copy(j, 5 + i, m_send.at[j, i], 2 * sgn).start()

    def finish(j):
        block = total[j, rows(0), :]
        for slot in (3, 4, 5, 6):
            block = block + landed(j, slot)
        for dx in range(NX):
            for c2 in range(NC):
                r = dx * 4 + c2 * 2
                t_send[dx, c2, j] = block[r : r + 2].astype(BF)
        g = j // PER
        if j % PER == PER - 1:
            for dx, dc in ALL:
                pltpu.make_async_remote_copy(
                    t_send.at[dx, lax.rem(c + dc, NC), pl.ds(g * PER, PER)],
                    t_recv.at[g, ((NX - dx) % NX) * NC + dc],
                    t_ssem, t_rsem.at[g], at(dx, 0, dc, -1), MESH,
                ).start()

    give(0)
    give(1)
    give(2)
    join(0)
    give(3)
    join(1)
    join(2)
    join(3)
    for j in range(J):
        merge(j)
    for j in range(J):
        finish(j)

    for copy in handed:
        copy.wait_recv()
    behind = saved_next[...].astype(F32)
    recip = recip_of(behind)
    unit = behind * recip
    for j in range(J):
        g, i = j // PER, j % PER
        if i == 0:
            pltpu.make_async_remote_copy(
                t_recv.at[g], t_recv.at[g], t_ssem, t_rsem.at[g], at(0, 0, 1), MESH
            ).wait_recv()
        for dc in range(NC):
            part = t_recv[g, dc, i].astype(F32)
            for dx in range(1, NX):
                part = part + t_recv[g, dx * NC + dc, i].astype(F32)
            dn[half(dc) + j] = part

    d_normed = jnp.concatenate([dn[k] for k in range(2 * J)], axis=1)
    scaled = gain_next[...].astype(F32) * d_normed
    grad = cot_next[0].astype(F32) + recip * (
        scaled - unit * jnp.mean(scaled * unit, axis=-1, keepdims=True)
    )
    out_ref[0] = grad.astype(BF)

    def drain(ref, sem):
        pltpu.make_async_copy(ref, ref, sem).wait()

    for copy in handed:
        copy.wait_send()
    drain(first.at[:, pl.ds(1, 7)], a_send)
    drain(x_buf.at[pl.ds(0, J), :, pl.ds(0, 7 * 16)], z_send)
    drain(x_buf.at[pl.ds(0, J)], sib_send)
    drain(pair_buf, pair_send)
    drain(r_recv, red_send)
    drain(t_recv, t_ssem)


def on_device(saved_in, grad_in, slot_table, gain, w_gate, w_up, w_down):
    d, hidden = w_gate.shape
    width = d // (2 * J)
    tokens = NX * NZ * NC * 2
    hbm = pl.BlockSpec(memory_space=pltpu.HBM)
    dma = pltpu.SemaphoreType.DMA
    row = (saved_in.shape[2], d)
    return pl.pallas_call(
        kernel,
        out_shape=jax.ShapeDtypeStruct(grad_in.shape, BF),
        in_specs=[hbm, hbm, pl.BlockSpec(memory_space=pltpu.SMEM), hbm, hbm, hbm, hbm],
        out_specs=pl.BlockSpec(memory_space=pltpu.VMEM),
        scratch_shapes=[
            pltpu.VMEM(saved_in.shape, BF),
            pltpu.VMEM(grad_in.shape, BF),
            pltpu.VMEM(gain.shape, BF),
            pltpu.VMEM(row, BF),
            pltpu.VMEM(row, BF),
            pltpu.VMEM(grad_in.shape, BF),
            pltpu.VMEM(gain.shape, BF),
            pltpu.VMEM((d, 2 * hidden), BF),
            pltpu.VMEM((hidden, d), BF),
            pltpu.VMEM((2 * J, 2, 2, width), BF),
            pltpu.VMEM((G, NX * NC, PER, 2, 2, width), BF),
            pltpu.VMEM((2 * J, 2, tokens, width), BF),
            pltpu.VMEM((tokens, 2 * hidden), F32),
            pltpu.VMEM((tokens, hidden), F32),
            pltpu.VMEM((tokens, 2 * hidden), BF),
            pltpu.VMEM((J, tokens, width), BF),
            pltpu.VMEM((J, tokens, width), BF),
            pltpu.VMEM((J, tokens, width), F32),
            pltpu.VMEM((J, tokens, width), BF),
            pltpu.VMEM((J, NZ - 1, 16, width), BF),
            pltpu.VMEM((J, 2, 16, width), BF),
            pltpu.VMEM((NX, NC, J, 2, width), BF),
            pltpu.VMEM((G, NX * NC, PER, 2, width), BF),
            pltpu.VMEM((2 * J, 2, width), F32),
            dma((3,)), dma((3,)), dma((3,)), dma((3,)),
            dma, dma((G,)), dma, dma((J, NZ)), dma, dma((J,)),
            dma, dma((J,)), dma, dma((J, NZ - 1)), dma, dma((G,)),
        ],
        compiler_params=pltpu.CompilerParams(
            collective_id=0, has_side_effects=True, vmem_limit_bytes=60 * 1024 * 1024
        ),
    )(saved_in, grad_in, slot_table, gain, w_gate, w_up, w_down)


def solution(mesh):
    return jax.shard_map(
        on_device,
        mesh=mesh,
        in_specs=(
            P("section", None, "seqtp", None),
            P("section", "seqtp", None),
            P("section"),
            P("section", None),
            P(None, "seqtp"),
            P(None, "seqtp"),
            P("seqtp", None),
        ),
        out_specs=P("section", "seqtp", None),
        check_vma=False,
    )
```
